32 devices in a mesh: dp: 8 (over z, y), section: 4 (over x, core).
Axes of the slice: x: 2, y: 2, z: 4, core: 2. Of those that a mesh axis runs over, the one named last changes fastest.
Arguments:
- inputs: bfloat16 [32, 532, 768], P(('dp', 'section')), may hold values from -6 to 6
- qkv_weight: bfloat16 [2, 768, 2304], replicated, may hold values from -0.21875 to 0.21875
- query_bias: bfloat16 [2, 768], replicated, may hold values from -3 to 3
- value_bias: bfloat16 [2, 768], replicated, may hold values from -0.59765625 to 0.59765625
- out_weight: bfloat16 [2, 768, 768], replicated, may hold values from -1.75 to 1.75
- out_bias: bfloat16 [2, 768], replicated, may hold values from -3 to 3
- norm1_gain: bfloat16 [2, 768], replicated, may hold values from 0.25 to 1.75
- norm1_shift: bfloat16 [2, 768], replicated, may hold values from -3 to 3
- up_weight: bfloat16 [2, 768, 3072], replicated, may hold values from -0.21875 to 0.21875
- up_bias: bfloat16 [2, 3072], replicated, may hold values from -3 to 3
- down_weight: bfloat16 [2, 3072, 768], replicated, may hold values from -0.109375 to 0.109375
- down_bias: bfloat16 [2, 768], replicated, may hold values from -3 to 3
- norm2_gain: bfloat16 [2, 768], replicated, may hold values from 0.25 to 1.75
- norm2_shift: bfloat16 [2, 768], replicated, may hold values from -3 to 3
- cotangent: bfloat16 [32, 80, 768], P(('dp', 'section')), may hold values from -6 to 6
- masked_rows: int32 [32, 80], P(('dp', 'section')), may hold values from 10 to 521
- row_valid: int32 [32, 80], P(('dp', 'section')), may hold values 0 or 1
Outputs:
- masked_out: bfloat16 [32, 80, 768], P(('dp', 'section'))
- input_grad: float32 [32, 532, 768], P(('dp', 'section'))
- grad_qkv: float32 [2, 768, 2304], P(None, 'dp')
- grad_query_bias: float32 [2, 768], P(None, 'dp')
- grad_value_bias: float32 [2, 768], P(None, 'dp')
- grad_out_weight: float32 [2, 768, 768], P(None, 'dp')
- grad_out_bias: float32 [2, 768], P(None, 'dp')
- grad_norm1_gain: float32 [2, 768], P(None, 'dp')
- grad_norm1_shift: float32 [2, 768], P(None, 'dp')
- grad_up_weight: float32 [2, 768, 3072], P(None, 'dp')
- grad_up_bias: float32 [2, 3072], P(None, 'dp')
- grad_down_weight: float32 [2, 3072, 768], P(None, 'dp')
- grad_down_bias: float32 [2, 768], P(None, 'dp')
- grad_norm2_gain: float32 [2, 768], P(None, 'dp')
- grad_norm2_shift: float32 [2, 768], P(None, 'dp')
The draws below stay inside these ranges and needn't reach their ends.
All inputs are finite; a program needn't handle non-finite values. No bound on the sum of `row_valid` on one device may be relied on, other than what follows from the above.
Results may differ from the reference program's by a relative error of at most 0.023.
Values may be sent and summed in bfloat16 or wider, within the bound.
No kernel may reach another device: no remote copies, remote signals or barrier semaphores. Data moves between devices by JAX's collectives and lax.ppermute only.
A program may use at most 320 MiB of HBM per device.

```python
from functools import partial
import jax
import jax.numpy as jnp
from jax import lax

D = 768
HEAD_DIM = 64
FF = 3072
LAYERS = 2
READ_MEM = 10
SEG_TOK = 512
MASKED = 80
ROWS = 532
SEGS = 32


def plant(values, key, low, high):
    longest = values.shape.index(max(values.shape))
    spots = []
    for shift in (0, 1):
        where = [jax.random.randint(jax.random.fold_in(key, axis), (), 0, length) for axis, length in enumerate(values.shape)]
        where[longest] = (where[longest] + shift) % values.shape[longest]
        spots.append(tuple(where))
    return values.at[spots[0]].set(low).at[spots[1]].set(high)


def raised(array, own_key, source, target, parts, factor):
    def block_of(axis_at):
        return (jnp.arange(array.shape[axis_at]) // (array.shape[axis_at] // parts)).reshape((-1,) + (1,) * (array.ndim - 1 - axis_at))

    near = jax.random.permutation(own_key, parts)[block_of(target)]
    other_side = (block_of(target) + parts // 2) % parts
    return jnp.where((block_of(source) == near) | (block_of(source) == other_side), factor * array, array)


def levels(own_key, dims, cuts, smallest, largest):
    level, own = 1.0, jax.random.fold_in(own_key, 6)
    for dim, shards_of in cuts:
        heights = jnp.exp(jax.random.uniform(jax.random.fold_in(own, dim), (shards_of,), jnp.float32, smallest / len(cuts), largest / len(cuts)))
        level = level * jnp.repeat(heights, dims[dim] // shards_of).reshape([-1 if axis == dim else 1 for axis in range(len(dims))])
    return level


def gaussian(key, dims, scale, bound, split=(), kind=jnp.bfloat16):
    values = jax.random.normal(key, dims, jnp.float32) * scale
    if len(split) > 0:
        values = levels(key, dims, split, -0.22, 0.18) * values
    return jnp.clip(values, min=-bound, max=bound).astype(kind)


def heavy_noise(key, extent, deviation, most, cuts, heavy, kind=jnp.bfloat16):
    result = deviation * jax.random.normal(key, extent, jnp.float32)
    if cuts:
        result = result * levels(key, extent, cuts, -0.22, 0.18)
    return jnp.clip(raised(result, jax.random.fold_in(key, 3), *heavy), -most, most).astype(kind)


def setup_inputs(seed: int = 0) -> dict:
    seeds = jax.random.split(jax.random.key(seed), 18)
    return {
        "inputs": heavy_noise(seeds[0], (SEGS, ROWS, D), 1.0, 6.0, ((0, 32),), (0, 2, 32, 2.75)),
        "qkv_weight": gaussian(seeds[1], (LAYERS, D, 3 * D), D ** -0.5, 0.21875),
        "query_bias": gaussian(seeds[2], (LAYERS, D), 0.5, 3.0),
        "value_bias": gaussian(seeds[3], (LAYERS, D), 0.1, 0.59765625),
        "out_weight": gaussian(seeds[4], (LAYERS, D, D), (D // 64) ** -0.5, 1.75),
        "out_bias": gaussian(seeds[5], (LAYERS, D), 0.5, 3.0),
        "norm1_gain": jnp.clip(1.0 + 0.15 * jax.random.normal(seeds[6], (LAYERS, D), jnp.float32), 0.25, 1.75).astype(jnp.bfloat16),
        "norm1_shift": gaussian(seeds[7], (LAYERS, D), 0.5, 3.0),
        "up_weight": gaussian(seeds[8], (LAYERS, D, FF), D ** -0.5, 0.21875),
        "up_bias": gaussian(seeds[9], (LAYERS, FF), 0.5, 3.0),
        "down_weight": gaussian(seeds[10], (LAYERS, FF, D), FF ** -0.5, 0.109375),
        "down_bias": gaussian(seeds[11], (LAYERS, D), 0.5, 3.0),
        "norm2_gain": jnp.clip(1.0 + 0.15 * jax.random.normal(seeds[12], (LAYERS, D), jnp.float32), 0.25, 1.75).astype(jnp.bfloat16),
        "norm2_shift": gaussian(seeds[13], (LAYERS, D), 0.5, 3.0),
        "cotangent": gaussian(seeds[14], (SEGS, MASKED, D), 1.0, 6.0, ((0, 32),)),
        "masked_rows": plant(jax.random.randint(seeds[15], (SEGS, MASKED), READ_MEM, READ_MEM + SEG_TOK), jax.random.fold_in(seeds[15], 1), READ_MEM, (READ_MEM + SEG_TOK) - 1).astype(jnp.int32),
        "row_valid": plant((jax.random.randint(seeds[16], (SEGS, MASKED), 0, 10) < 9).astype(jnp.int32), jax.random.fold_in(seeds[16], 1), 0, 1),
    }


EPS = 1e-06
HIGH = lax.Precision.HIGHEST

@jax.custom_vjp
def low(v):
    return lax.optimization_barrier(v.astype(jnp.bfloat16)).astype(jnp.float32)

@jax.custom_vjp
def low_back(v):
    return v

def low_keep(v):
    return (low(v), None)

def low_pass(kept, grad):
    return (grad,)

def back_keep(v):
    return (v, None)

def back_low(kept, grad):
    return (low(grad),)
low.defvjp(low_keep, low_pass)
low_back.defvjp(back_keep, back_low)

def layer_norm(resid, norm_gain, norm_shift):
    centre = lax.optimization_barrier(jnp.mean(resid, -1, keepdims=True))
    offset = resid - centre
    spread = lax.optimization_barrier(jnp.mean(offset * offset, -1, keepdims=True))
    return offset * lax.rsqrt(spread + EPS) * norm_gain + norm_shift

def exact_gelu(pre_values):
    return jax.nn.gelu(pre_values, approximate=False)

def matmul(left, right):
    return jnp.dot(left, right, precision=HIGH, preferred_element_type=jnp.float32)

def layer_forward(hidden, params):
    qkv_weight, query_bias, value_bias, out_weight, out_bias, norm1_gain, norm1_shift, up_weight, up_bias, down_weight, down_bias, norm2_gain, norm2_shift = params
    row_count, model_width = hidden.shape
    head_count = model_width // HEAD_DIM
    score_scale = HEAD_DIM ** (-0.5)
    projected = matmul(hidden, qkv_weight)
    queries = low_back(low(projected[:, :model_width] + query_bias)).reshape(row_count, head_count, HEAD_DIM)
    key_rows = low_back(low(projected[:, model_width:2 * model_width])).reshape(row_count, head_count, HEAD_DIM)
    value_rows = low_back(low(projected[:, 2 * model_width:] + value_bias)).reshape(row_count, head_count, HEAD_DIM)
    scores = low_back(jnp.einsum('qhd,khd->hqk', queries, key_rows, precision=HIGH) * score_scale)
    softmax_low = low(jax.nn.softmax(scores, axis=-1))
    mixed_rows = jnp.einsum('hqk,khd->qhd', softmax_low, value_rows, precision=HIGH).reshape(row_count, model_width)
    attended = low_back(low(mixed_rows))
    branch = low_back(matmul(attended, out_weight) + out_bias)
    first_norm = layer_norm(hidden + branch, norm1_gain, norm1_shift)
    up_pre = low_back(matmul(low(first_norm), up_weight) + up_bias)
    activated = low(exact_gelu(up_pre))
    second_branch = low_back(matmul(activated, down_weight) + down_bias)
    return layer_norm(first_norm + second_branch, norm2_gain, norm2_shift)

def layer_params(params_all, layer_index):
    return tuple((stacked[layer_index] for stacked in params_all))

def segment_forward(seg_inputs, params_all, selector):
    boundary = low_back(low(layer_forward(seg_inputs, layer_params(params_all, 0))))
    top_out = layer_forward(boundary, layer_params(params_all, 1))
    return matmul(selector, low(top_out))

def add_pair(first_term, second_term):
    return first_term + second_term

def reference(inputs, qkv_weight, query_bias, value_bias, out_weight, out_bias, norm1_gain, norm1_shift, up_weight, up_bias, down_weight, down_bias, norm2_gain, norm2_shift, cotangent, masked_rows, row_valid):
    params_all = tuple((stacked.astype(jnp.float32) for stacked in (qkv_weight, query_bias, value_bias, out_weight, out_bias, norm1_gain, norm1_shift, up_weight, up_bias, down_weight, down_bias, norm2_gain, norm2_shift)))
    positions = jnp.arange(ROWS, dtype=jnp.int32)
    selectors = (masked_rows[:, :, None].astype(jnp.int32) == positions).astype(jnp.float32) * row_valid[:, :, None].astype(jnp.float32)

    def per_segment(totals, packed):
        seg_inputs, seg_selector, seg_cot = packed
        outputs, pullback = jax.vjp(partial(segment_forward, selector=seg_selector), seg_inputs, params_all)
        d_inputs, d_params = pullback(seg_cot)
        totals = jax.tree.map(add_pair, totals, d_params)
        return (totals, (outputs.astype(jnp.bfloat16), d_inputs))
    zero_totals = tuple((jnp.zeros_like(stacked) for stacked in params_all))
    totals, (masked_out, input_grad) = lax.scan(per_segment, zero_totals, (inputs.astype(jnp.float32), selectors, cotangent.astype(jnp.float32)))
    return (masked_out, input_grad, totals[0], totals[1], totals[2], totals[3], totals[4], totals[5], totals[6], totals[7], totals[8], totals[9], totals[10], totals[11], totals[12])
```

```python
import jax
import jax.numpy as jnp
from jax import lax
from jax.sharding import PartitionSpec as P

HEAD_DIM = 64
EPS = 1e-06
BF = jnp.bfloat16
F32 = jnp.float32


def dot(left, right, left_dim=1, right_dim=0):
    return lax.dot_general(
        left, right, (((left_dim,), (right_dim,)), ((), ())), preferred_element_type=F32
    )


def norm_parts(resid):
    centre = jnp.mean(resid, -1, keepdims=True)
    offset = resid - centre
    spread = jnp.mean(offset * offset, -1, keepdims=True)
    scale = lax.rsqrt(spread + EPS)
    return offset * scale, scale


def norm_back(grad, normed, scale, gain):
    inner = grad * gain
    mean_inner = jnp.mean(inner, -1, keepdims=True)
    mean_prod = jnp.mean(inner * normed, -1, keepdims=True)
    d_resid = scale * (inner - mean_inner - normed * mean_prod)
    return d_resid, jnp.sum(grad * normed, 0), jnp.sum(grad, 0)


def gelu_pair(pre):
    cdf = 0.5 * lax.erfc(-pre * (0.5**0.5))
    density = jnp.exp(-0.5 * pre * pre) * ((0.5 / jnp.pi) ** 0.5)
    return pre * cdf, cdf + pre * density


def heads_of(rows):
    return rows.reshape(rows.shape[0], -1, HEAD_DIM)


def attention_forward(queries, keys, values):
    scores = (
        jnp.einsum("qhd,khd->hqk", heads_of(queries), heads_of(keys), preferred_element_type=F32)
        * HEAD_DIM**-0.5
    )
    probs = jax.nn.softmax(scores, axis=-1)
    attended = jnp.einsum(
        "hqk,khd->qhd", probs.astype(BF), heads_of(values), preferred_element_type=F32
    )
    return probs, attended.reshape(queries.shape).astype(BF)


def attention_backward(queries, keys, values, probs, d_attended):
    scale = HEAD_DIM**-0.5
    d_att = heads_of(d_attended)
    d_probs = jnp.einsum("qhd,khd->hqk", d_att, heads_of(values), preferred_element_type=F32)
    d_values = jnp.einsum("hqk,qhd->khd", probs.astype(BF), d_att, preferred_element_type=F32)
    row_terms = jnp.sum(probs * d_probs, -1, keepdims=True)
    d_scores = (probs * (d_probs - row_terms)).astype(BF)
    d_queries = jnp.einsum("hqk,khd->qhd", d_scores, heads_of(keys), preferred_element_type=F32)
    d_keys = jnp.einsum("hqk,qhd->khd", d_scores, heads_of(queries), preferred_element_type=F32)
    return (
        (d_queries * scale).reshape(queries.shape).astype(BF),
        (d_keys * scale).reshape(keys.shape).astype(BF),
        d_values.reshape(values.shape).astype(BF),
    )


def tail_forward(hidden, attended, par):
    first_sum = hidden.astype(F32) + (dot(attended, par["out_weight"]) + par["out_bias"])
    normed1, scale1 = norm_parts(first_sum)
    first_norm = normed1 * par["norm1_gain"] + par["norm1_shift"]
    first_low = first_norm.astype(BF)
    up_pre = dot(first_low, par["up_weight"]) + par["up_bias"]
    act, slope = gelu_pair(up_pre)
    act = act.astype(BF)
    second_sum = first_norm + (dot(act, par["down_weight"]) + par["down_bias"])
    normed2, scale2 = norm_parts(second_sum)
    layer_out = normed2 * par["norm2_gain"] + par["norm2_shift"]
    return layer_out.astype(BF), (normed1, scale1, first_low, slope.astype(BF), act, normed2, scale2)


def tail_backward(grad_out, attended, saved, par):
    normed1, scale1, first_low, slope, act, normed2, scale2 = saved
    d_second, g_gain2, g_shift2 = norm_back(grad_out, normed2, scale2, par["norm2_gain"])
    d_down = d_second.astype(BF)
    d_up = (slope.astype(F32) * dot(d_down, par["down_weight"], 1, 1)).astype(BF)
    d_first_norm = d_second + dot(d_up, par["up_weight"], 1, 1)
    d_first, g_gain1, g_shift1 = norm_back(d_first_norm, normed1, scale1, par["norm1_gain"])
    d_branch = d_first.astype(BF)
    d_attended = dot(d_branch, par["out_weight"], 1, 1).astype(BF)
    small = {
        "norm2_gain": g_gain2,
        "norm2_shift": g_shift2,
        "down_bias": jnp.sum(d_down.astype(F32), 0),
        "up_bias": jnp.sum(d_up.astype(F32), 0),
        "norm1_gain": g_gain1,
        "norm1_shift": g_shift1,
        "out_bias": jnp.sum(d_branch.astype(F32), 0),
    }
    g_down = dot(act, d_down, 0, 0).astype(BF)
    g_up = dot(first_low, d_up, 0, 0).astype(BF)
    g_out = dot(attended, d_branch, 0, 0).astype(BF)
    return d_first, d_attended, (g_down, g_up, g_out), small


NAMES = (
    "qkv_weight",
    "query_bias",
    "value_bias",
    "out_weight",
    "out_bias",
    "norm1_gain",
    "norm1_shift",
    "up_weight",
    "up_bias",
    "down_weight",
    "down_bias",
    "norm2_gain",
    "norm2_shift",
)
SMALL = tuple(name for name in NAMES if not name.endswith("weight"))


def swap(value, axis, bit):
    size = lax.axis_size(axis)
    return lax.ppermute(value, axis, [(i, i ^ bit) for i in range(size)])


def bit_of(axis, bit):
    return (lax.axis_index(axis) // bit) % 2


def halve(value, axis, bit, dim):
    mine = bit_of(axis, bit)
    kept = lax.dynamic_index_in_dim(value, mine, dim, keepdims=False)
    sent = lax.dynamic_index_in_dim(value, 1 - mine, dim, keepdims=False)
    got = swap(sent, axis, bit)
    return (kept.astype(F32) + got.astype(F32)).astype(value.dtype)


def double(value, axis, bit, dim):
    got = swap(value, axis, bit)
    mine = bit_of(axis, bit)
    low = jnp.where(mine == 0, value, got)
    high = jnp.where(mine == 0, got, value)
    return jnp.stack([low, high], dim)


def reduce_blocks(grad):
    blocks = lax.axis_size("dp")
    rows, columns = grad.shape
    part = rows // blocks
    value = halve(grad.reshape(rows, 2, columns // 2), "section", 1, 1)
    value = value.reshape(blocks, 2, part // 2, columns // 2)
    value = halve(value, "section", 2, 1)
    bit = 1
    while bit < blocks:
        left = value.shape[0]
        value = halve(value.reshape(left // 2, 2, part // 2, columns // 2), "dp", bit, 1)
        bit *= 2
    value = value.reshape(part // 2, columns // 2)
    value = double(value, "section", 2, 0).reshape(part, columns // 2)
    return double(value, "section", 1, 1).reshape(part, columns)


def side_by_side(grad, blocks):
    rows, columns = grad.shape
    return grad.reshape(blocks, 4, rows // (4 * blocks), columns).swapaxes(1, 2).reshape(rows // 4, 4 * columns)


def one_above_another(block, columns):
    rows = block.shape[0]
    return block.reshape(rows, 4, columns).swapaxes(0, 1).reshape(4 * rows, columns)


def reduce_small(vectors):
    blocks = lax.axis_size("dp")
    packed = jnp.concatenate([v.reshape(blocks, -1) for v in vectors], 1)
    packed = packed + swap(packed, "section", 1)
    packed = packed + swap(packed, "section", 2)
    bit = 1
    while bit < blocks:
        packed = halve(packed.reshape(packed.shape[0] // 2, 2, -1), "dp", bit, 1)
        bit *= 2
    packed = packed.reshape(-1)
    pieces, at = [], 0
    for v in vectors:
        width = v.shape[0] // blocks
        pieces.append(packed[at : at + width])
        at += width
    return pieces


def local(inputs, *rest):
    weights = dict(zip(NAMES, rest[: len(NAMES)]))
    cotangent, masked_rows, row_valid = (value[0] for value in rest[len(NAMES) :])
    params = []
    for layer in range(2):
        params.append(
            {
                name: stacked[layer] if stacked.ndim == 3 else stacked[layer].astype(F32)
                for name, stacked in weights.items()
            }
        )
    par0, par1 = params
    hidden = inputs[0]
    rows, width = hidden.shape
    blocks = lax.axis_size("dp")

    projected = dot(hidden, par0["qkv_weight"])
    q0 = (projected[:, :width] + par0["query_bias"]).astype(BF)
    k0 = projected[:, width : 2 * width].astype(BF)
    v0 = (projected[:, 2 * width :] + par0["value_bias"]).astype(BF)
    probs0, att0 = attention_forward(q0, k0, v0)
    boundary, saved0 = tail_forward(hidden, att0, par0)

    pick = (masked_rows[:, None] == jnp.arange(rows, dtype=jnp.int32)).astype(BF)
    valid = row_valid.astype(F32)[:, None]
    slots = dot(pick, boundary).astype(BF)
    key_value = dot(boundary, par1["qkv_weight"][:, width:])
    q1 = (dot(slots, par1["qkv_weight"][:, :width]) + par1["query_bias"]).astype(BF)
    k1 = key_value[:, :width].astype(BF)
    v1 = (key_value[:, width:] + par1["value_bias"]).astype(BF)
    probs1, att1 = attention_forward(q1, k1, v1)
    top, saved1 = tail_forward(slots, att1, par1)
    masked_out = (top.astype(F32) * valid).astype(BF)

    top_grad = cotangent.astype(F32) * valid
    d_first1, d_att1, big1, small1 = tail_backward(top_grad, att1, saved1, par1)
    down1, up1, out1 = big1
    ff1 = reduce_blocks(jnp.concatenate([up1, side_by_side(down1, blocks)], 1))
    d_q1, d_k1, d_v1 = attention_backward(q1, k1, v1, probs1, d_att1)
    small1["query_bias"] = jnp.sum(d_q1.astype(F32), 0)
    small1["value_bias"] = jnp.sum(d_v1.astype(F32), 0)
    d_kv1 = jnp.concatenate([d_k1, d_v1], 1)
    qkv1 = jnp.concatenate([dot(slots, d_q1, 0, 0), dot(boundary, d_kv1, 0, 0)], 1).astype(BF)
    at1 = reduce_blocks(jnp.concatenate([qkv1, out1], 1))
    d_slots = d_first1 + dot(d_q1, par1["qkv_weight"][:, :width], 1, 1)
    slots_hi = d_slots.astype(BF)
    slots_lo = (d_slots - slots_hi.astype(F32)).astype(BF)
    d_boundary = (
        dot(d_kv1, par1["qkv_weight"][:, width:], 1, 1)
        + dot(pick, slots_hi, 0, 0)
        + dot(pick, slots_lo, 0, 0)
    )
    bound_grad = d_boundary.astype(BF).astype(F32)

    d_first0, d_att0, big0, small0 = tail_backward(bound_grad, att0, saved0, par0)
    down0, up0, out0 = big0
    ff0 = reduce_blocks(jnp.concatenate([up0, side_by_side(down0, blocks)], 1))
    d_q0, d_k0, d_v0 = attention_backward(q0, k0, v0, probs0, d_att0)
    small0["query_bias"] = jnp.sum(d_q0.astype(F32), 0)
    small0["value_bias"] = jnp.sum(d_v0.astype(F32), 0)
    d_proj0 = jnp.concatenate([d_q0, d_k0, d_v0], 1)
    qkv0 = dot(hidden, d_proj0, 0, 0).astype(BF)
    at0 = reduce_blocks(jnp.concatenate([qkv0, out0], 1))
    input_grad = d_first0 + dot(d_proj0, par0["qkv_weight"], 1, 1)

    vectors = reduce_small([small[name] for small in (small0, small1) for name in SMALL])
    count = len(SMALL)
    result = {name: jnp.stack([vectors[i], vectors[count + i]]) for i, name in enumerate(SMALL)}
    ff_width = par0["up_weight"].shape[1]
    result["up_weight"] = jnp.stack([ff[:, :ff_width] for ff in (ff0, ff1)]).astype(F32)
    result["down_weight"] = jnp.stack(
        [one_above_another(ff[:, ff_width:], width) for ff in (ff0, ff1)]
    ).astype(F32)
    result["qkv_weight"] = jnp.stack([at[:, : 3 * width] for at in (at0, at1)]).astype(F32)
    result["out_weight"] = jnp.stack([at[:, 3 * width :] for at in (at0, at1)]).astype(F32)
    return (masked_out[None], input_grad[None]) + tuple(result[name] for name in NAMES)


def solution(mesh):
    both = ("dp", "section")
    wide, flat = P(None, "dp", None), P(None, "dp")
    return jax.shard_map(
        local,
        mesh=mesh,
        in_specs=(P(both, None, None),)
        + (P(),) * len(NAMES)
        + (P(both, None, None), P(both, None), P(both, None)),
        out_specs=(P(both, None, None), P(both, None, None))
        + tuple(wide if name.endswith("weight") else flat for name in NAMES),
        check_vma=False,
    )
```
